128 devices in a mesh: shard: 32 (over z, x, core), tensor: 4 (over y).
Axes of the slice: x: 4, y: 4, z: 4, core: 2. Of those that a mesh axis runs over, the one named last changes fastest.
Arguments:
- weights: float32 [48, 640, 1280], P(None, 'shard', 'tensor'), may hold values from -40 to 40
- grads: bfloat16 [48, 640, 1280], P(None, 'shard', 'tensor'), may hold values from -13 to 13
- owner_slot: int32 [96], replicated, may hold values from 0 to 255, as said below
- left_stats: float32 [256, 640, 640], P(('shard', 'tensor')), may hold values from -0.15 to 2, as said below
- right_stats: float32 [256, 640, 640], P(('shard', 'tensor')), may hold values from -0.15 to 2, as said below
- left_root: bfloat16 [256, 640, 640], P(('shard', 'tensor')), may hold values from -0.15 to 1.5, as said below
- right_root: bfloat16 [256, 640, 640], P(('shard', 'tensor')), may hold values from -0.15 to 1.5, as said below
- moment: float32 [256, 640, 640], P(('shard', 'tensor')), may hold values from 1e-05 to 0.001
Outputs:
- new_weights: float32 [48, 640, 1280], P(None, 'shard', 'tensor')
- new_left: float32 [256, 640, 640], P(('shard', 'tensor'))
- new_right: float32 [256, 640, 640], P(('shard', 'tensor'))
- new_moment: float32 [256, 640, 640], P(('shard', 'tensor'))
The draws below stay inside these ranges and needn't reach their ends.
Inputs may be any that keep to these rules, and one draw needn't show every extreme that they name: `owner_slot`: the values are distinct; the slots g with g // 2 equal to one device are that device's, and some device holds 2 blocks in every draw. `left_stats`: Symmetric. `right_stats`: Symmetric. `left_root`: Symmetric. `right_root`: Symmetric.
All inputs are finite; a program needn't handle non-finite values.
Results may differ from the reference program's by a relative error of at most 0.0017.
Values may be sent and summed in bfloat16 or wider, within the bound.
A program may use at most 128 MiB of HBM per device.

```python
import math
import jax
import jax.numpy as jnp
from jax import lax

D = 1280
BLK = 640
SLOTS = 2
GSLOTS = 256
NROWB = 48
NCB = 2
NBLK = 96


def square_matrix(key, low, high, spread):
    first, second = jax.random.split(key)
    diag_vals = jnp.exp(jax.random.uniform(first, (GSLOTS, 1, BLK), jnp.float32, math.log(low), math.log(high)))
    noise = jax.random.truncated_normal(second, -3.0, 3.0, (GSLOTS, BLK, BLK), jnp.float32) * spread
    offdiag = (noise + jnp.swapaxes(noise, 1, 2)) * 0.5
    square = jnp.arange(BLK)[:, None] == jnp.arange(BLK)[None, :]
    return jnp.where(square[None, :, :], diag_vals, offdiag)


def draw_left_stats(key, part):
    return square_matrix(jax.random.fold_in(key, 21), 0.5, 2.0, 0.02)


def draw_right_stats(key, part):
    return square_matrix(jax.random.fold_in(key, 22), 0.5, 2.0, 0.02)


def draw_left_root(key, part):
    return square_matrix(jax.random.fold_in(key, 23), 0.5, 1.5, 0.02).astype(jnp.bfloat16)


def draw_right_root(key, part):
    return square_matrix(jax.random.fold_in(key, 24), 0.5, 1.5, 0.02).astype(jnp.bfloat16)


def draw_weights(key, part):
    first, second = jax.random.split(jax.random.fold_in(key, 31))
    column = jnp.arange(D).astype(jnp.float32) / (D - 1)
    random_scale = jnp.exp(jax.random.uniform(first, (1, 1, D), jnp.float32, 0.0, math.log(2.0)))
    scale = jnp.exp(column * math.log(3.0))[None, None, :] * random_scale
    noise = jax.random.truncated_normal(second, -4.0, 4.0, (NROWB, BLK, D), jnp.float32)
    return noise * scale


def draw_grads(key, part):
    first, second, third = jax.random.split(jax.random.fold_in(key, 41), 3)
    row_scale = jnp.exp(jax.random.uniform(first, (NROWB, BLK, 1), jnp.float32, 0.0, math.log(10.0)))
    col_scale = jnp.exp(jax.random.uniform(second, (1, 1, D), jnp.float32, 0.0, math.log(10.0)))
    noise = jax.random.truncated_normal(third, -4.0, 4.0, (NROWB, BLK, D), jnp.float32)
    return (0.003 * row_scale * col_scale * noise).astype(jnp.bfloat16)


def draw_owner_slot(key, part):
    first, second = jax.random.split(jax.random.fold_in(key, 51))
    order = jax.random.permutation(first, GSLOTS).astype(jnp.int32)
    leader = order[0] // SLOTS
    ranking = (order // SLOTS != leader).astype(jnp.int32)
    ranked = order[jnp.argsort(ranking, stable=True)]
    chosen = ranked[:NBLK]
    spread = jax.random.permutation(second, NBLK)
    return chosen[spread].astype(jnp.int32)


def shard_levels(rng, dims, cuts, low, largest):
    def one(position, parts):
        draws = jax.random.uniform(jax.random.fold_in(jax.random.fold_in(rng, 6), position), (parts,), jnp.float32, low / len(cuts), largest / len(cuts))
        return jnp.repeat(jnp.exp(draws), dims[position] // parts).reshape((-1,) + (1,) * (len(dims) - position - 1))

    gain = one(*cuts[0])
    for cut in cuts[1:]:
        gain = gain * one(*cut)
    return gain


def setup_inputs(seed: int = 0) -> dict:
    seeds = jax.random.split(jax.random.key(seed), 9)
    return {
        "weights": draw_weights(jax.random.fold_in(seeds[8], 71), 0),
        "grads": draw_grads(jax.random.fold_in(seeds[8], 71), 0),
        "owner_slot": draw_owner_slot(jax.random.fold_in(seeds[8], 71), 0),
        "left_stats": draw_left_stats(jax.random.fold_in(seeds[8], 71), 0),
        "right_stats": draw_right_stats(jax.random.fold_in(seeds[8], 71), 0),
        "left_root": draw_left_root(jax.random.fold_in(seeds[8], 71), 0),
        "right_root": draw_right_root(jax.random.fold_in(seeds[8], 71), 0),
        "moment": jnp.clip(jnp.exp(math.log(0.001) - 4.6051703 * jax.random.uniform(seeds[7], (GSLOTS, BLK, BLK), jnp.float32) ** shard_levels(seeds[7], (GSLOTS, BLK, BLK), ((0, 128),), -0.2, 0.2)), 9.999999747378752e-06, 0.001),
    }


stat_decay = 0.9
step_size = 0.2

def slot_update(items):
    grad, left, right, left_inv, right_inv, second = items
    gram_left = jnp.dot(grad, grad.T, preferred_element_type=jnp.float32)
    gram_right = jnp.dot(grad.T, grad, preferred_element_type=jnp.float32)
    new_left = stat_decay * left + (1.0 - stat_decay) * gram_left
    new_right = stat_decay * right + (1.0 - stat_decay) * gram_right
    half = jnp.dot(left_inv, grad, preferred_element_type=jnp.float32).astype(jnp.bfloat16)
    precond = jnp.dot(half, right_inv, preferred_element_type=jnp.float32)
    grad_full = grad.astype(jnp.float32)
    new_second = stat_decay * second + (1.0 - stat_decay) * grad_full * grad_full
    adam = grad_full / (jnp.sqrt(new_second) + 1e-08)
    graft = jnp.sqrt(jnp.mean(adam * adam)) / jnp.sqrt(jnp.mean(precond * precond) + 1e-06)
    delta = (graft * precond).astype(jnp.bfloat16)
    return (new_left, new_right, new_second, delta)

def reference(weights, grads, owner_slot, left_stats, right_stats, left_root, right_root, moment):
    blocks = grads.reshape(NROWB, BLK, NCB, BLK).transpose(0, 2, 1, 3).reshape(NBLK, BLK, BLK)
    slot_grads = jnp.zeros((GSLOTS, BLK, BLK), grads.dtype).at[owner_slot].set(blocks)
    new_left, new_right, new_moment, deltas = lax.map(slot_update, (slot_grads, left_stats, right_stats, left_root, right_root, moment))
    placed = deltas[owner_slot].reshape(NROWB, NCB, BLK, BLK).transpose(0, 2, 1, 3).reshape(NROWB, BLK, D)
    updated = weights - step_size * placed.astype(jnp.float32)
    new_weights = updated * lax.rsqrt(lax.optimization_barrier(jnp.mean(updated * updated, axis=2, keepdims=True)) + 1e-06)
    return (new_weights, new_left, new_right, new_moment)
```

```python
import jax
import jax.numpy as jnp
from jax import lax
from jax.sharding import PartitionSpec as P

stat_decay = 0.9
step_size = 0.2


def route_out(outgoing):
    arrived = lax.all_to_all(outgoing, ("shard", "tensor"), split_axis=0, concat_axis=0, tiled=True)
    return arrived


def route_back(outgoing):
    arrived = lax.all_to_all(outgoing, ("shard", "tensor"), split_axis=0, concat_axis=0, tiled=True)
    return arrived


def refresh(block_grads, left_stats, right_stats):
    gram_left = jnp.einsum(
        "kij,klj->kil", block_grads, block_grads, preferred_element_type=jnp.float32
    )
    gram_right = jnp.einsum(
        "kji,kjl->kil", block_grads, block_grads, preferred_element_type=jnp.float32
    )
    new_left = stat_decay * left_stats + (1.0 - stat_decay) * gram_left
    new_right = stat_decay * right_stats + (1.0 - stat_decay) * gram_right
    return (new_left, new_right)


def direction(block_grads, left_root, right_root, moment):
    half = jnp.einsum(
        "kij,kjl->kil", left_root, block_grads, preferred_element_type=jnp.float32
    ).astype(jnp.bfloat16)
    precond = jnp.einsum("kij,kjl->kil", half, right_root, preferred_element_type=jnp.float32)
    grad_full = block_grads.astype(jnp.float32)
    new_moment = stat_decay * moment + (1.0 - stat_decay) * grad_full * grad_full
    adam = grad_full / (jnp.sqrt(new_moment) + 1e-08)
    graft = jnp.sqrt(jnp.mean(adam * adam, axis=(1, 2))) / jnp.sqrt(
        jnp.mean(precond * precond, axis=(1, 2)) + 1e-06
    )
    delta = (graft[:, None, None] * precond).astype(jnp.bfloat16)
    return (delta, new_moment)


def body(weights, grads, owner_slot, left_stats, right_stats, left_root, right_root, moment):
    n_shard = lax.axis_size("shard")
    n_tensor = lax.axis_size("tensor")
    row_blocks, shard_rows, shard_cols = grads.shape
    order_size = left_stats.shape[1]
    width = shard_cols * n_tensor
    col_blocks = width // order_size
    per_block = n_tensor // col_blocks
    slots = left_stats.shape[0]
    owners = n_shard * n_tensor
    total_slots = owners * slots
    half = shard_rows // col_blocks
    mine_col = lax.axis_index("tensor") // per_block
    partner = [(i, (i + per_block) % n_tensor) for i in range(n_tensor)]
    keep = lax.dynamic_slice_in_dim(grads, mine_col * half, half, axis=1)
    give = lax.dynamic_slice_in_dim(grads, (1 - mine_col) * half, half, axis=1)
    got = lax.ppermute(give, "tensor", partner)
    first = jnp.where(mine_col == 0, keep, got)
    second = jnp.where(mine_col == 0, got, keep)
    slabs = jnp.stack([first, second], axis=1).reshape(row_blocks * col_blocks, half, shard_cols)
    outgoing = jnp.zeros((total_slots, half, shard_cols), jnp.bfloat16).at[owner_slot].set(slabs)
    arrived = route_out(outgoing)
    arrived = arrived.reshape(n_shard, col_blocks, per_block, slots, half, shard_cols)
    block_grads = arrived.transpose(3, 0, 1, 4, 2, 5).reshape(slots, order_size, order_size)
    new_left, new_right = refresh(block_grads, left_stats, right_stats)
    delta, new_moment = direction(block_grads, left_root, right_root, moment)
    pieces = delta.reshape(slots, n_shard, col_blocks, half, per_block, shard_cols).transpose(
        1, 2, 4, 0, 3, 5
    )
    sendback = pieces.reshape(total_slots, half, shard_cols)
    returned = route_back(sendback)
    back = returned[owner_slot].reshape(row_blocks, col_blocks, half, shard_cols)
    own_part = jnp.where(mine_col == 0, back[:, 0], back[:, 1])
    other_part = jnp.where(mine_col == 0, back[:, 1], back[:, 0])
    other_back = lax.ppermute(other_part, "tensor", partner)
    top = jnp.where(mine_col == 0, own_part, other_back)
    bottom = jnp.where(mine_col == 0, other_back, own_part)
    my_delta = jnp.concatenate([top, bottom], axis=1)
    updated = weights - step_size * my_delta.astype(jnp.float32)
    squares = lax.psum(jnp.sum(updated * updated, axis=2), "tensor")
    new_weights = updated * lax.rsqrt(squares / width + 1e-06)[:, :, None]
    return (new_weights, new_left, new_right, new_moment)


def solution(mesh):
    placed = (
        P(None, "shard", "tensor"),
        P(None, "shard", "tensor"),
        P(),
        P(("shard", "tensor"), None, None),
        P(("shard", "tensor"), None, None),
        P(("shard", "tensor"), None, None),
        P(("shard", "tensor"), None, None),
        P(("shard", "tensor"), None, None),
    )
    return jax.shard_map(
        body,
        mesh=mesh,
        in_specs=placed,
        out_specs=(
            P(None, "shard", "tensor"),
            P(("shard", "tensor"), None, None),
            P(("shard", "tensor"), None, None),
            P(("shard", "tensor"), None, None),
        ),
        check_vma=False,
    )
```

```python
import jax
import jax.numpy as jnp
from jax import lax
from jax.sharding import PartitionSpec as P

stat_decay = 0.9
step_size = 0.2


def route_out(outgoing):
    n_shard = lax.axis_size("shard")
    n_tensor = lax.axis_size("tensor")
    staged = outgoing.reshape((n_shard, n_tensor, -1) + outgoing.shape[1:])
    staged = lax.all_to_all(staged, "shard", split_axis=0, concat_axis=0, tiled=True)
    arrived = lax.all_to_all(staged, "tensor", split_axis=1, concat_axis=1, tiled=True)
    return arrived.reshape(outgoing.shape)


def route_back(outgoing):
    return route_out(outgoing)


def refresh(block_grads, left_stats, right_stats):
    gram_left = jnp.einsum(
        "kij,klj->kil", block_grads, block_grads, preferred_element_type=jnp.float32
    )
    gram_right = jnp.einsum(
        "kji,kjl->kil", block_grads, block_grads, preferred_element_type=jnp.float32
    )
    new_left = stat_decay * left_stats + (1.0 - stat_decay) * gram_left
    new_right = stat_decay * right_stats + (1.0 - stat_decay) * gram_right
    return (new_left, new_right)


def direction(block_grads, left_root, right_root, moment):
    half = jnp.einsum(
        "kij,kjl->kil", left_root, block_grads, preferred_element_type=jnp.float32
    ).astype(jnp.bfloat16)
    precond = jnp.einsum("kij,kjl->kil", half, right_root, preferred_element_type=jnp.float32)
    grad_full = block_grads.astype(jnp.float32)
    new_moment = stat_decay * moment + (1.0 - stat_decay) * grad_full * grad_full
    adam = grad_full / (jnp.sqrt(new_moment) + 1e-08)
    graft = jnp.sqrt(jnp.mean(adam * adam, axis=(1, 2))) / jnp.sqrt(
        jnp.mean(precond * precond, axis=(1, 2)) + 1e-06
    )
    delta = (graft[:, None, None] * precond).astype(jnp.bfloat16)
    return (delta, new_moment)


def body(weights, grads, owner_slot, left_stats, right_stats, left_root, right_root, moment):
    n_shard = lax.axis_size("shard")
    n_tensor = lax.axis_size("tensor")
    row_blocks, shard_rows, shard_cols = grads.shape
    order_size = left_stats.shape[1]
    width = shard_cols * n_tensor
    col_blocks = width // order_size
    per_block = n_tensor // col_blocks
    slots = left_stats.shape[0]
    owners = n_shard * n_tensor
    total_slots = owners * slots
    half = shard_rows // col_blocks
    mine_col = lax.axis_index("tensor") // per_block
    partner = [(i, (i + per_block) % n_tensor) for i in range(n_tensor)]
    keep = lax.dynamic_slice_in_dim(grads, mine_col * half, half, axis=1)
    give = lax.dynamic_slice_in_dim(grads, (1 - mine_col) * half, half, axis=1)
    got = lax.ppermute(give, "tensor", partner)
    first = jnp.where(mine_col == 0, keep, got)
    second = jnp.where(mine_col == 0, got, keep)
    slabs = jnp.stack([first, second], axis=1).reshape(row_blocks * col_blocks, half, shard_cols)
    outgoing = jnp.zeros((total_slots, half, shard_cols), jnp.bfloat16).at[owner_slot].set(slabs)
    arrived = route_out(outgoing)
    arrived = arrived.reshape(n_shard, col_blocks, per_block, slots, half, shard_cols)
    block_grads = arrived.transpose(3, 0, 1, 4, 2, 5).reshape(slots, order_size, order_size)
    new_left, new_right = refresh(block_grads, left_stats, right_stats)
    delta, new_moment = direction(block_grads, left_root, right_root, moment)
    pieces = delta.reshape(slots, n_shard, col_blocks, half, per_block, shard_cols).transpose(
        1, 2, 4, 0, 3, 5
    )
    sendback = pieces.reshape(total_slots, half, shard_cols)
    returned = route_back(sendback)
    back = returned[owner_slot].reshape(row_blocks, col_blocks, half, shard_cols)
    own_part = jnp.where(mine_col == 0, back[:, 0], back[:, 1])
    other_part = jnp.where(mine_col == 0, back[:, 1], back[:, 0])
    other_back = lax.ppermute(other_part, "tensor", partner)
    top = jnp.where(mine_col == 0, own_part, other_back)
    bottom = jnp.where(mine_col == 0, other_back, own_part)
    my_delta = jnp.concatenate([top, bottom], axis=1)
    updated = weights - step_size * my_delta.astype(jnp.float32)
    squares = lax.psum(jnp.sum(updated * updated, axis=2), "tensor")
    new_weights = updated * lax.rsqrt(squares / width + 1e-06)[:, :, None]
    return (new_weights, new_left, new_right, new_moment)


def solution(mesh):
    placed = (
        P(None, "shard", "tensor"),
        P(None, "shard", "tensor"),
        P(),
        P(("shard", "tensor"), None, None),
        P(("shard", "tensor"), None, None),
        P(("shard", "tensor"), None, None),
        P(("shard", "tensor"), None, None),
        P(("shard", "tensor"), None, None),
    )
    return jax.shard_map(
        body,
        mesh=mesh,
        in_specs=placed,
        out_specs=(
            P(None, "shard", "tensor"),
            P(("shard", "tensor"), None, None),
            P(("shard", "tensor"), None, None),
            P(("shard", "tensor"), None, None),
        ),
        check_vma=False,
    )
```

```python
import jax
import jax.numpy as jnp
from jax import lax
from jax.sharding import PartitionSpec as P

stat_decay = 0.9
step_size = 0.2


def route_out(outgoing):
    arrived = lax.all_to_all(outgoing, ("shard", "tensor"), split_axis=0, concat_axis=0, tiled=True)
    return arrived


def route_back(outgoing):
    arrived = lax.all_to_all(outgoing, ("shard", "tensor"), split_axis=0, concat_axis=0, tiled=True)
    return arrived


def refresh(block_grads, left_stats, right_stats):
    gram_left = jnp.einsum(
        "kij,klj->kil", block_grads, block_grads, preferred_element_type=jnp.float32
    )
    gram_right = jnp.einsum(
        "kji,kjl->kil", block_grads, block_grads, preferred_element_type=jnp.float32
    )
    new_left = stat_decay * left_stats + (1.0 - stat_decay) * gram_left
    new_right = stat_decay * right_stats + (1.0 - stat_decay) * gram_right
    return (new_left, new_right)


def direction(block_grads, left_root, right_root, moment):
    half = jnp.einsum(
        "kij,kjl->kil", left_root, block_grads, preferred_element_type=jnp.float32
    ).astype(jnp.bfloat16)
    precond = jnp.einsum("kij,kjl->kil", half, right_root, preferred_element_type=jnp.float32)
    grad_full = block_grads.astype(jnp.float32)
    new_moment = stat_decay * moment + (1.0 - stat_decay) * grad_full * grad_full
    adam = grad_full / (jnp.sqrt(new_moment) + 1e-08)
    graft = jnp.sqrt(jnp.mean(adam * adam, axis=(1, 2))) / jnp.sqrt(
        jnp.mean(precond * precond, axis=(1, 2)) + 1e-06
    )
    delta = (graft[:, None, None] * precond).astype(jnp.bfloat16)
    return (delta, new_moment)


def body(weights, grads, owner_slot, left_stats, right_stats, left_root, right_root, moment):
    n_shard = lax.axis_size("shard")
    n_tensor = lax.axis_size("tensor")
    row_blocks, shard_rows, shard_cols = grads.shape
    order_size = left_stats.shape[1]
    width = shard_cols * n_tensor
    col_blocks = width // order_size
    per_block = n_tensor // col_blocks
    slots = left_stats.shape[0]
    owners = n_shard * n_tensor
    total_slots = owners * slots
    half = shard_rows // col_blocks
    mine_col = lax.axis_index("tensor") // per_block
    partner = [(i, (i + per_block) % n_tensor) for i in range(n_tensor)]
    keep = lax.dynamic_slice_in_dim(grads, mine_col * half, half, axis=1)
    give = lax.dynamic_slice_in_dim(grads, (1 - mine_col) * half, half, axis=1)
    got = lax.ppermute(give, "tensor", partner)
    first = jnp.where(mine_col == 0, keep, got)
    second = jnp.where(mine_col == 0, got, keep)
    slabs = jnp.stack([first, second], axis=1).reshape(row_blocks * col_blocks, half, shard_cols)
    outgoing = jnp.zeros((total_slots, half, shard_cols), jnp.bfloat16).at[owner_slot].set(slabs)
    arrived = route_out(outgoing)
    arrived = arrived.reshape(n_shard, col_blocks, per_block, slots, half, shard_cols)
    block_grads = arrived.transpose(3, 0, 1, 4, 2, 5).reshape(slots, order_size, order_size)
    new_left, new_right = refresh(block_grads, left_stats, right_stats)
    delta, new_moment = direction(block_grads, left_root, right_root, moment)
    pieces = delta.reshape(slots, n_shard, col_blocks, half, per_block, shard_cols).transpose(
        1, 2, 4, 0, 3, 5
    )
    sendback = pieces.reshape(total_slots, half, shard_cols)
    returned = route_back(sendback)
    back = returned[owner_slot].reshape(row_blocks, col_blocks, half, shard_cols)
    own_part = jnp.where(mine_col == 0, back[:, 0], back[:, 1])
    other_part = jnp.where(mine_col == 0, back[:, 1], back[:, 0])
    other_back = lax.ppermute(other_part, "tensor", partner)
    top = jnp.where(mine_col == 0, own_part, other_back)
    bottom = jnp.where(mine_col == 0, other_back, own_part)
    my_delta = jnp.concatenate([top, bottom], axis=1)
    updated = weights - step_size * my_delta.astype(jnp.float32)
    squares = jnp.sum(updated * updated, axis=2)
    step = 1
    while step < n_tensor:
        pairs = [(i, i ^ step) for i in range(n_tensor)]
        squares = squares + lax.ppermute(squares, "tensor", pairs)
        step *= 2
    new_weights = updated * lax.rsqrt(squares / width + 1e-06)[:, :, None]
    return (new_weights, new_left, new_right, new_moment)


def solution(mesh):
    placed = (
        P(None, "shard", "tensor"),
        P(None, "shard", "tensor"),
        P(),
        P(("shard", "tensor"), None, None),
        P(("shard", "tensor"), None, None),
        P(("shard", "tensor"), None, None),
        P(("shard", "tensor"), None, None),
        P(("shard", "tensor"), None, None),
    )
    return jax.shard_map(
        body,
        mesh=mesh,
        in_specs=placed,
        out_specs=(
            P(None, "shard", "tensor"),
            P(("shard", "tensor"), None, None),
            P(("shard", "tensor"), None, None),
            P(("shard", "tensor"), None, None),
        ),
        check_vma=False,
    )
```

```python
import jax
import jax.numpy as jnp
from jax import lax
from jax.sharding import PartitionSpec as P

stat_decay = 0.9
step_size = 0.2


def route_out(outgoing):
    arrived = lax.all_to_all(outgoing, ("shard", "tensor"), split_axis=0, concat_axis=0, tiled=True)
    return arrived


def route_back(outgoing):
    arrived = lax.all_to_all(outgoing, ("shard", "tensor"), split_axis=0, concat_axis=0, tiled=True)
    return arrived


def refresh(block_grads, left_stats, right_stats):
    gram_left = jnp.einsum(
        "kij,klj->kil", block_grads, block_grads, preferred_element_type=jnp.float32
    )
    gram_right = jnp.einsum(
        "kji,kjl->kil", block_grads, block_grads, preferred_element_type=jnp.float32
    )
    new_left = stat_decay * left_stats + (1.0 - stat_decay) * gram_left
    new_right = stat_decay * right_stats + (1.0 - stat_decay) * gram_right
    return (new_left, new_right)


def direction(block_grads, left_root, right_root, moment):
    half = jnp.einsum(
        "kij,kjl->kil", left_root, block_grads, preferred_element_type=jnp.float32
    ).astype(jnp.bfloat16)
    precond = jnp.einsum("kij,kjl->kil", half, right_root, preferred_element_type=jnp.float32)
    grad_full = block_grads.astype(jnp.float32)
    new_moment = stat_decay * moment + (1.0 - stat_decay) * grad_full * grad_full
    adam = grad_full / (jnp.sqrt(new_moment) + 1e-08)
    graft = jnp.sqrt(jnp.mean(adam * adam, axis=(1, 2))) / jnp.sqrt(
        jnp.mean(precond * precond, axis=(1, 2)) + 1e-06
    )
    delta = (graft[:, None, None] * precond).astype(jnp.bfloat16)
    return (delta, new_moment)


def body(weights, grads, owner_slot, left_stats, right_stats, left_root, right_root, moment):
    n_shard = lax.axis_size("shard")
    n_tensor = lax.axis_size("tensor")
    row_blocks, shard_rows, shard_cols = grads.shape
    order_size = left_stats.shape[1]
    width = shard_cols * n_tensor
    col_blocks = width // order_size
    per_block = n_tensor // col_blocks
    slots = left_stats.shape[0]
    owners = n_shard * n_tensor
    total_slots = owners * slots
    half = shard_rows // col_blocks
    mine_col = lax.axis_index("tensor") // per_block
    partner = [(i, (i + per_block) % n_tensor) for i in range(n_tensor)]
    keep = lax.dynamic_slice_in_dim(grads, mine_col * half, half, axis=1)
    give = lax.dynamic_slice_in_dim(grads, (1 - mine_col) * half, half, axis=1)
    got = lax.ppermute(give, "tensor", partner)
    first = jnp.where(mine_col == 0, keep, got)
    second = jnp.where(mine_col == 0, got, keep)
    block_count = owner_slot.shape[0]
    slab_size = half * shard_cols
    chunk = slots * slab_size
    lanes = 128 if chunk % 128 == 0 else chunk
    slabs = jnp.stack([first, second], axis=1).reshape(row_blocks * col_blocks, slab_size)
    slot_block = jnp.zeros((total_slots,), jnp.int32).at[owner_slot].set(
        jnp.arange(block_count, dtype=jnp.int32)
    )
    slot_used = jnp.zeros((total_slots,), jnp.bool_).at[owner_slot].set(True)
    outgoing = jnp.where(slot_used[:, None], slabs[slot_block], jnp.zeros((), jnp.bfloat16))
    arrived = route_out(outgoing.reshape(owners, chunk // lanes, lanes))
    arrived = arrived.reshape(n_shard, col_blocks, per_block, slots, half, shard_cols)
    block_grads = arrived.transpose(3, 0, 1, 4, 2, 5).reshape(slots, order_size, order_size)
    new_left, new_right = refresh(block_grads, left_stats, right_stats)
    delta, new_moment = direction(block_grads, left_root, right_root, moment)
    pieces = delta.reshape(slots, n_shard, col_blocks, half, per_block, shard_cols).transpose(
        1, 2, 4, 0, 3, 5
    )
    sendback = pieces.reshape(owners, chunk // lanes, lanes)
    returned = route_back(sendback).reshape(total_slots, slab_size)
    back = returned[owner_slot].reshape(row_blocks, col_blocks, half, shard_cols)
    own_part = jnp.where(mine_col == 0, back[:, 0], back[:, 1])
    other_part = jnp.where(mine_col == 0, back[:, 1], back[:, 0])
    other_back = lax.ppermute(other_part, "tensor", partner)
    top = jnp.where(mine_col == 0, own_part, other_back)
    bottom = jnp.where(mine_col == 0, other_back, own_part)
    my_delta = jnp.concatenate([top, bottom], axis=1)
    updated = weights - step_size * my_delta.astype(jnp.float32)
    squares = jnp.sum(updated * updated, axis=2)
    step = 1
    while step < n_tensor:
        pairs = [(i, i ^ step) for i in range(n_tensor)]
        squares = squares + lax.ppermute(squares, "tensor", pairs)
        step *= 2
    new_weights = updated * lax.rsqrt(squares / width + 1e-06)[:, :, None]
    return (new_weights, new_left, new_right, new_moment)


def solution(mesh):
    placed = (
        P(None, "shard", "tensor"),
        P(None, "shard", "tensor"),
        P(),
        P(("shard", "tensor"), None, None),
        P(("shard", "tensor"), None, None),
        P(("shard", "tensor"), None, None),
        P(("shard", "tensor"), None, None),
        P(("shard", "tensor"), None, None),
    )
    return jax.shard_map(
        body,
        mesh=mesh,
        in_specs=placed,
        out_specs=(
            P(None, "shard", "tensor"),
            P(("shard", "tensor"), None, None),
            P(("shard", "tensor"), None, None),
            P(("shard", "tensor"), None, None),
        ),
        check_vma=False,
    )
```

```python
import jax
import jax.numpy as jnp
from jax import lax
from jax.sharding import PartitionSpec as P

stat_decay = 0.9
step_size = 0.2


def route_out(outgoing):
    arrived = lax.all_to_all(outgoing, ("shard", "tensor"), split_axis=0, concat_axis=0, tiled=True)
    return arrived


def route_back(outgoing):
    arrived = lax.all_to_all(outgoing, ("shard", "tensor"), split_axis=0, concat_axis=0, tiled=True)
    return arrived


def refresh(block_grads, left_stats, right_stats):
    gram_left = jnp.einsum(
        "kij,klj->kil", block_grads, block_grads, preferred_element_type=jnp.float32
    )
    gram_right = jnp.einsum(
        "kji,kjl->kil", block_grads, block_grads, preferred_element_type=jnp.float32
    )
    new_left = stat_decay * left_stats + (1.0 - stat_decay) * gram_left
    new_right = stat_decay * right_stats + (1.0 - stat_decay) * gram_right
    return (new_left, new_right)


def direction(block_grads, left_root, right_root, moment):
    half = jnp.einsum(
        "kij,kjl->kil", left_root, block_grads, preferred_element_type=jnp.float32
    ).astype(jnp.bfloat16)
    precond = jnp.einsum("kij,kjl->kil", half, right_root, preferred_element_type=jnp.float32)
    grad_full = block_grads.astype(jnp.float32)
    new_moment = stat_decay * moment + (1.0 - stat_decay) * grad_full * grad_full
    adam = grad_full / (jnp.sqrt(new_moment) + 1e-08)
    graft = jnp.sqrt(jnp.mean(adam * adam, axis=(1, 2))) / jnp.sqrt(
        jnp.mean(precond * precond, axis=(1, 2)) + 1e-06
    )
    delta = (graft[:, None, None] * precond).astype(jnp.bfloat16)
    return (delta, new_moment)


def body(weights, grads, owner_slot, left_stats, right_stats, left_root, right_root, moment):
    n_shard = lax.axis_size("shard")
    n_tensor = lax.axis_size("tensor")
    row_blocks, shard_rows, shard_cols = grads.shape
    order_size = left_stats.shape[1]
    width = shard_cols * n_tensor
    col_blocks = width // order_size
    per_block = n_tensor // col_blocks
    slots = left_stats.shape[0]
    owners = n_shard * n_tensor
    total_slots = owners * slots
    quarter = shard_rows // n_tensor
    block_count = owner_slot.shape[0]
    slab_size = quarter * order_size
    chunk = slots * slab_size
    lanes = 128 if chunk % 128 == 0 else chunk
    parts = grads.reshape(row_blocks, n_tensor, quarter, shard_cols)
    parts = lax.all_to_all(parts, "tensor", split_axis=1, concat_axis=1, tiled=True)
    rows = parts.reshape(row_blocks, col_blocks, per_block, quarter, shard_cols).transpose(0, 1, 3, 2, 4)
    slabs = rows.reshape(row_blocks * col_blocks, slab_size)
    slot_block = jnp.zeros((total_slots,), jnp.int32).at[owner_slot].set(
        jnp.arange(block_count, dtype=jnp.int32)
    )
    slot_used = jnp.zeros((total_slots,), jnp.bool_).at[owner_slot].set(True)
    outgoing = jnp.where(slot_used[:, None], slabs[slot_block], jnp.zeros((), jnp.bfloat16))
    arrived = route_out(outgoing.reshape(owners, chunk // lanes, lanes))
    arrived = arrived.reshape(owners, slots, quarter, order_size)
    block_grads = arrived.transpose(1, 0, 2, 3).reshape(slots, order_size, order_size)
    new_left, new_right = refresh(block_grads, left_stats, right_stats)
    delta, new_moment = direction(block_grads, left_root, right_root, moment)
    pieces = delta.reshape(slots, owners, quarter, order_size).transpose(1, 0, 2, 3)
    sendback = pieces.reshape(owners, chunk // lanes, lanes)
    returned = route_back(sendback).reshape(total_slots, slab_size)
    back = returned[owner_slot].reshape(row_blocks, col_blocks, quarter, per_block, shard_cols)
    back = back.transpose(0, 1, 3, 2, 4).reshape(row_blocks, n_tensor, quarter, shard_cols)
    back = lax.all_to_all(back, "tensor", split_axis=1, concat_axis=1, tiled=True)
    my_delta = back.reshape(row_blocks, shard_rows, shard_cols)
    updated = weights - step_size * my_delta.astype(jnp.float32)
    squares = jnp.sum(updated * updated, axis=2)
    step = 1
    while step < n_tensor:
        pairs = [(i, i ^ step) for i in range(n_tensor)]
        squares = squares + lax.ppermute(squares, "tensor", pairs)
        step *= 2
    new_weights = updated * lax.rsqrt(squares / width + 1e-06)[:, :, None]
    return (new_weights, new_left, new_right, new_moment)


def solution(mesh):
    placed = (
        P(None, "shard", "tensor"),
        P(None, "shard", "tensor"),
        P(),
        P(("shard", "tensor"), None, None),
        P(("shard", "tensor"), None, None),
        P(("shard", "tensor"), None, None),
        P(("shard", "tensor"), None, None),
        P(("shard", "tensor"), None, None),
    )
    return jax.shard_map(
        body,
        mesh=mesh,
        in_specs=placed,
        out_specs=(
            P(None, "shard", "tensor"),
            P(("shard", "tensor"), None, None),
            P(("shard", "tensor"), None, None),
            P(("shard", "tensor"), None, None),
        ),
        check_vma=False,
    )
```

```python
import jax
import jax.numpy as jnp
from jax import lax
from jax.sharding import PartitionSpec as P

stat_decay = 0.9
step_size = 0.2


def route_out(outgoing):
    arrived = lax.all_to_all(outgoing, ("shard", "tensor"), split_axis=0, concat_axis=0, tiled=True)
    return arrived


def route_back(outgoing):
    arrived = lax.all_to_all(outgoing, ("shard", "tensor"), split_axis=0, concat_axis=0, tiled=True)
    return arrived


def refresh(block_grads, left_stats, right_stats):
    gram_left = jnp.einsum(
        "kij,klj->kil", block_grads, block_grads, preferred_element_type=jnp.float32
    )
    new_left = stat_decay * left_stats + (1.0 - stat_decay) * gram_left
    gram_right = jnp.einsum(
        "kji,kjl->kil", block_grads, block_grads, preferred_element_type=jnp.float32
    )
    new_right = stat_decay * right_stats + (1.0 - stat_decay) * gram_right
    return (new_left, new_right)


def direction(block_grads, left_root, right_root, moment):
    half = jnp.einsum(
        "kij,kjl->kil", left_root, block_grads, preferred_element_type=jnp.float32
    ).astype(jnp.bfloat16)
    precond = jnp.einsum("kij,kjl->kil", half, right_root, preferred_element_type=jnp.float32)
    grad_full = block_grads.astype(jnp.float32)
    new_moment = stat_decay * moment + (1.0 - stat_decay) * grad_full * grad_full
    adam = grad_full / (jnp.sqrt(new_moment) + 1e-08)
    graft = jnp.sqrt(jnp.mean(adam * adam, axis=(1, 2))) / jnp.sqrt(
        jnp.mean(precond * precond, axis=(1, 2)) + 1e-06
    )
    delta = (graft[:, None, None] * precond).astype(jnp.bfloat16)
    return (delta, new_moment)


def body_steps(weights, grads, owner_slot, left_stats, right_stats, left_root, right_root, moment):
    n_shard = lax.axis_size("shard")
    n_tensor = lax.axis_size("tensor")
    row_blocks, shard_rows, shard_cols = grads.shape
    order_size = left_stats.shape[1]
    width = shard_cols * n_tensor
    col_blocks = width // order_size
    per_block = n_tensor // col_blocks
    slots = left_stats.shape[0]
    owners = n_shard * n_tensor
    total_slots = owners * slots
    half = shard_rows // col_blocks
    mine_col = lax.axis_index("tensor") // per_block
    partner = [(i, (i + per_block) % n_tensor) for i in range(n_tensor)]
    keep = lax.dynamic_slice_in_dim(grads, mine_col * half, half, axis=1)
    give = lax.dynamic_slice_in_dim(grads, (1 - mine_col) * half, half, axis=1)
    got = lax.ppermute(give, "tensor", partner)
    first = jnp.where(mine_col == 0, keep, got)
    second = jnp.where(mine_col == 0, got, keep)
    block_count = owner_slot.shape[0]
    slab_size = half * shard_cols
    chunk = slots * slab_size
    lanes = 128 if chunk % 128 == 0 else chunk
    slabs = jnp.stack([first, second], axis=1).reshape(row_blocks * col_blocks, slab_size)
    slot_block = jnp.zeros((total_slots,), jnp.int32).at[owner_slot].set(
        jnp.arange(block_count, dtype=jnp.int32)
    )
    slot_used = jnp.zeros((total_slots,), jnp.bool_).at[owner_slot].set(True)
    outgoing = jnp.where(slot_used[:, None], slabs[slot_block], jnp.zeros((), jnp.bfloat16))
    arrived = route_out(outgoing.reshape(owners, chunk // lanes, lanes))
    arrived = arrived.reshape(n_shard, col_blocks, per_block, slots, half, shard_cols)
    block_grads = arrived.transpose(3, 0, 1, 4, 2, 5).reshape(slots, order_size, order_size)
    new_left, new_right = refresh(block_grads, left_stats, right_stats)
    delta, new_moment = direction(block_grads, left_root, right_root, moment)
    pieces = delta.reshape(slots, n_shard, col_blocks, half, per_block, shard_cols).transpose(
        1, 2, 4, 0, 3, 5
    )
    sendback = pieces.reshape(owners, chunk // lanes, lanes)
    returned = route_back(sendback).reshape(total_slots, slab_size)
    back = returned[owner_slot].reshape(row_blocks, col_blocks, half, shard_cols)
    own_part = jnp.where(mine_col == 0, back[:, 0], back[:, 1])
    other_part = jnp.where(mine_col == 0, back[:, 1], back[:, 0])
    other_back = lax.ppermute(other_part, "tensor", partner)
    top = jnp.where(mine_col == 0, own_part, other_back)
    bottom = jnp.where(mine_col == 0, other_back, own_part)
    my_delta = jnp.concatenate([top, bottom], axis=1)
    updated = weights - step_size * my_delta.astype(jnp.float32)
    partial = jnp.sum(updated * updated, axis=2)
    shifted = [partial] + [
        lax.ppermute(partial, "tensor", [(i, (i + k) % n_tensor) for i in range(n_tensor)])
        for k in range(1, n_tensor)
    ]
    ranked = jnp.stack(shifted[:1] + shifted[:0:-1])
    ranked = jnp.roll(ranked, lax.axis_index("tensor"), axis=0)
    while ranked.shape[0] > 1:
        ranked = ranked[0::2] + ranked[1::2]
    squares = ranked[0]
    new_weights = updated * lax.rsqrt(squares / width + 1e-06)[:, :, None]
    return (new_weights, new_left, new_right, new_moment)


def solution(mesh):
    placed = (
        P(None, "shard", "tensor"),
        P(None, "shard", "tensor"),
        P(),
        P(("shard", "tensor"), None, None),
        P(("shard", "tensor"), None, None),
        P(("shard", "tensor"), None, None),
        P(("shard", "tensor"), None, None),
        P(("shard", "tensor"), None, None),
    )
    return jax.shard_map(
        body_steps,
        mesh=mesh,
        in_specs=placed,
        out_specs=(
            P(None, "shard", "tensor"),
            P(("shard", "tensor"), None, None),
            P(("shard", "tensor"), None, None),
            P(("shard", "tensor"), None, None),
        ),
        check_vma=False,
    )
```

```python
import jax
import jax.numpy as jnp
from jax import lax
from jax.sharding import PartitionSpec as P

stat_decay = 0.9
step_size = 0.2


def route_out(outgoing):
    arrived = lax.all_to_all(outgoing, ("shard", "tensor"), split_axis=0, concat_axis=0, tiled=True)
    return arrived


def route_back(outgoing):
    arrived = lax.all_to_all(outgoing, ("shard", "tensor"), split_axis=0, concat_axis=0, tiled=True)
    return arrived


def refresh(block_grads, left_stats, right_stats):
    gram_left = jnp.einsum(
        "kij,klj->kil", block_grads, block_grads, preferred_element_type=jnp.float32
    )
    new_left = stat_decay * left_stats + (1.0 - stat_decay) * gram_left
    gram_right = jnp.einsum(
        "kji,kjl->kil", block_grads, block_grads, preferred_element_type=jnp.float32
    )
    new_right = stat_decay * right_stats + (1.0 - stat_decay) * gram_right
    return (new_left, new_right)


def direction(block_grads, left_root, right_root, moment):
    half = jnp.einsum(
        "kij,kjl->kil", left_root, block_grads, preferred_element_type=jnp.float32
    ).astype(jnp.bfloat16)
    precond = jnp.einsum("kij,kjl->kil", half, right_root, preferred_element_type=jnp.float32)
    grad_full = block_grads.astype(jnp.float32)
    new_moment = stat_decay * moment + (1.0 - stat_decay) * grad_full * grad_full
    adam = grad_full / (jnp.sqrt(new_moment) + 1e-08)
    graft = jnp.sqrt(jnp.mean(adam * adam, axis=(1, 2))) / jnp.sqrt(
        jnp.mean(precond * precond, axis=(1, 2)) + 1e-06
    )
    delta = (graft[:, None, None] * precond).astype(jnp.bfloat16)
    return (delta, new_moment)


def body_steps(weights, grads, owner_slot, left_stats, right_stats, left_root, right_root, moment):
    n_shard = lax.axis_size("shard")
    n_tensor = lax.axis_size("tensor")
    row_blocks, shard_rows, shard_cols = grads.shape
    order_size = left_stats.shape[1]
    width = shard_cols * n_tensor
    col_blocks = width // order_size
    per_block = n_tensor // col_blocks
    slots = left_stats.shape[0]
    owners = n_shard * n_tensor
    total_slots = owners * slots
    half = shard_rows // col_blocks
    mine_col = lax.axis_index("tensor") // per_block
    partner = [(i, (i + per_block) % n_tensor) for i in range(n_tensor)]
    keep = lax.dynamic_slice_in_dim(grads, mine_col * half, half, axis=1)
    give = lax.dynamic_slice_in_dim(grads, (1 - mine_col) * half, half, axis=1)
    got = lax.ppermute(give, "tensor", partner)
    first = jnp.where(mine_col == 0, keep, got)
    second = jnp.where(mine_col == 0, got, keep)
    block_count = owner_slot.shape[0]
    slab_size = half * shard_cols
    chunk = slots * slab_size
    lanes = 128 if chunk % 128 == 0 else chunk
    slabs = jnp.stack([first, second], axis=1).reshape(row_blocks * col_blocks, slab_size)
    slot_block = jnp.full((total_slots,), block_count, jnp.int32).at[owner_slot].set(
        jnp.arange(block_count, dtype=jnp.int32)
    )
    slabs = jnp.concatenate([slabs, jnp.zeros((1, slab_size), jnp.bfloat16)], axis=0)
    outgoing = slabs[slot_block]
    arrived = route_out(outgoing.reshape(owners, chunk // lanes, lanes))
    arrived = arrived.reshape(n_shard, col_blocks, per_block, slots, half, shard_cols)
    block_grads = arrived.transpose(3, 0, 1, 4, 2, 5).reshape(slots, order_size, order_size)
    new_left, new_right = refresh(block_grads, left_stats, right_stats)
    delta, new_moment = direction(block_grads, left_root, right_root, moment)
    pieces = delta.reshape(slots, n_shard, col_blocks, half, per_block, shard_cols).transpose(
        1, 2, 4, 0, 3, 5
    )
    sendback = pieces.reshape(owners, chunk // lanes, lanes)
    returned = route_back(sendback).reshape(total_slots, slab_size)
    back = returned[owner_slot].reshape(row_blocks, col_blocks, half, shard_cols)
    own_part = jnp.where(mine_col == 0, back[:, 0], back[:, 1])
    other_part = jnp.where(mine_col == 0, back[:, 1], back[:, 0])
    other_back = lax.ppermute(other_part, "tensor", partner)
    top = jnp.where(mine_col == 0, own_part, other_back)
    bottom = jnp.where(mine_col == 0, other_back, own_part)
    my_delta = jnp.concatenate([top, bottom], axis=1)
    updated = weights - step_size * my_delta.astype(jnp.float32)
    squares = jnp.sum(updated * updated, axis=2)
    step = 1
    while step < n_tensor:
        pairs = [(i, i ^ step) for i in range(n_tensor)]
        squares = squares + lax.ppermute(squares, "tensor", pairs)
        step *= 2
    new_weights = updated * lax.rsqrt(squares / width + 1e-06)[:, :, None]
    return (new_weights, new_left, new_right, new_moment)


def solution(mesh):
    placed = (
        P(None, "shard", "tensor"),
        P(None, "shard", "tensor"),
        P(),
        P(("shard", "tensor"), None, None),
        P(("shard", "tensor"), None, None),
        P(("shard", "tensor"), None, None),
        P(("shard", "tensor"), None, None),
        P(("shard", "tensor"), None, None),
    )
    return jax.shard_map(
        body_steps,
        mesh=mesh,
        in_specs=placed,
        out_specs=(
            P(None, "shard", "tensor"),
            P(("shard", "tensor"), None, None),
            P(("shard", "tensor"), None, None),
            P(("shard", "tensor"), None, None),
        ),
        check_vma=False,
    )
```

```python
import jax
import jax.numpy as jnp
from jax import lax
from jax.sharding import PartitionSpec as P

stat_decay = 0.9
step_size = 0.2


def route_out(outgoing):
    arrived = lax.all_to_all(outgoing, ("shard", "tensor"), split_axis=0, concat_axis=0, tiled=True)
    return arrived


def route_back(outgoing):
    arrived = lax.all_to_all(outgoing, ("shard", "tensor"), split_axis=0, concat_axis=0, tiled=True)
    return arrived


def refresh(block_grads, left_stats, right_stats):
    gram_left = jnp.einsum(
        "kij,klj->kil", block_grads, block_grads, preferred_element_type=jnp.float32
    )
    new_left = stat_decay * left_stats + (1.0 - stat_decay) * gram_left
    gram_right = jnp.einsum(
        "kji,kjl->kil", block_grads, block_grads, preferred_element_type=jnp.float32
    )
    new_right = stat_decay * right_stats + (1.0 - stat_decay) * gram_right
    return (new_left, new_right)


def direction(block_grads, left_root, right_root, moment):
    half = jnp.einsum(
        "kij,kjl->kil", left_root, block_grads, preferred_element_type=jnp.float32
    ).astype(jnp.bfloat16)
    precond = jnp.einsum("kij,kjl->kil", half, right_root, preferred_element_type=jnp.float32)
    grad_full = block_grads.astype(jnp.float32)
    new_moment = stat_decay * moment + (1.0 - stat_decay) * grad_full * grad_full
    adam = grad_full / (jnp.sqrt(new_moment) + 1e-08)
    graft = jnp.sqrt(jnp.mean(adam * adam, axis=(1, 2))) / jnp.sqrt(
        jnp.mean(precond * precond, axis=(1, 2)) + 1e-06
    )
    delta = (graft[:, None, None] * precond).astype(jnp.bfloat16)
    return (delta, new_moment)


def body_steps(weights, grads, owner_slot, left_stats, right_stats, left_root, right_root, moment):
    n_shard = lax.axis_size("shard")
    n_tensor = lax.axis_size("tensor")
    row_blocks, shard_rows, shard_cols = grads.shape
    order_size = left_stats.shape[1]
    width = shard_cols * n_tensor
    col_blocks = width // order_size
    per_block = n_tensor // col_blocks
    slots = left_stats.shape[0]
    owners = n_shard * n_tensor
    total_slots = owners * slots
    half = shard_rows // col_blocks
    mine_col = lax.axis_index("tensor") // per_block
    partner = [(i, n_tensor - 1 - i) for i in range(n_tensor)]
    keep = lax.dynamic_slice_in_dim(grads, mine_col * half, half, axis=1)
    give = lax.dynamic_slice_in_dim(grads, (1 - mine_col) * half, half, axis=1)
    got = lax.ppermute(give, "tensor", partner)
    first = jnp.where(mine_col == 0, keep, got)
    second = jnp.where(mine_col == 0, got, keep)
    block_count = owner_slot.shape[0]
    slab_size = half * shard_cols
    chunk = slots * slab_size
    lanes = 128 if chunk % 128 == 0 else chunk
    slabs = jnp.stack([first, second], axis=1).reshape(row_blocks * col_blocks, slab_size)
    slot_block = jnp.zeros((total_slots,), jnp.int32).at[owner_slot].set(
        jnp.arange(block_count, dtype=jnp.int32)
    )
    slot_used = jnp.zeros((total_slots,), jnp.bool_).at[owner_slot].set(True)
    outgoing = jnp.where(slot_used[:, None], slabs[slot_block], jnp.zeros((), jnp.bfloat16))
    arrived = route_out(outgoing.reshape(owners, chunk // lanes, lanes))
    arrived = arrived.reshape(n_shard, col_blocks, per_block, slots, half, shard_cols)
    my_slots = lax.axis_index(("shard", "tensor")) * slots + jnp.arange(slots)
    slot_col = slot_block[my_slots] % col_blocks
    flip = (jnp.arange(col_blocks)[:, None] != slot_col[None, :])[None, :, None, :, None, None]
    arrived = jnp.where(flip, arrived[:, :, ::-1], arrived)
    block_grads = arrived.transpose(3, 0, 1, 4, 2, 5).reshape(slots, order_size, order_size)
    new_left, new_right = refresh(block_grads, left_stats, right_stats)
    delta, new_moment = direction(block_grads, left_root, right_root, moment)
    pieces = delta.reshape(slots, n_shard, col_blocks, half, per_block, shard_cols).transpose(
        1, 2, 4, 0, 3, 5
    )
    pieces = jnp.where(flip, pieces[:, :, ::-1], pieces)
    sendback = pieces.reshape(owners, chunk // lanes, lanes)
    returned = route_back(sendback).reshape(total_slots, slab_size)
    back = returned[owner_slot].reshape(row_blocks, col_blocks, half, shard_cols)
    own_part = jnp.where(mine_col == 0, back[:, 0], back[:, 1])
    other_part = jnp.where(mine_col == 0, back[:, 1], back[:, 0])
    other_back = lax.ppermute(other_part, "tensor", partner)
    top = jnp.where(mine_col == 0, own_part, other_back)
    bottom = jnp.where(mine_col == 0, other_back, own_part)
    my_delta = jnp.concatenate([top, bottom], axis=1)
    updated = weights - step_size * my_delta.astype(jnp.float32)
    squares = jnp.sum(updated * updated, axis=2)
    step = 1
    while step < n_tensor:
        pairs = [(i, i ^ step) for i in range(n_tensor)]
        squares = squares + lax.ppermute(squares, "tensor", pairs)
        step *= 2
    new_weights = updated * lax.rsqrt(squares / width + 1e-06)[:, :, None]
    return (new_weights, new_left, new_right, new_moment)


def solution(mesh):
    placed = (
        P(None, "shard", "tensor"),
        P(None, "shard", "tensor"),
        P(),
        P(("shard", "tensor"), None, None),
        P(("shard", "tensor"), None, None),
        P(("shard", "tensor"), None, None),
        P(("shard", "tensor"), None, None),
        P(("shard", "tensor"), None, None),
    )
    return jax.shard_map(
        body_steps,
        mesh=mesh,
        in_specs=placed,
        out_specs=(
            P(None, "shard", "tensor"),
            P(("shard", "tensor"), None, None),
            P(("shard", "tensor"), None, None),
            P(("shard", "tensor"), None, None),
        ),
        check_vma=False,
    )
```

```python
import jax
import jax.numpy as jnp
from jax import lax
from jax.sharding import PartitionSpec as P

stat_decay = 0.9
step_size = 0.2


def route_out(outgoing):
    arrived = lax.all_to_all(outgoing, ("shard", "tensor"), split_axis=0, concat_axis=0, tiled=True)
    return arrived


def route_back(outgoing):
    arrived = lax.all_to_all(outgoing, ("shard", "tensor"), split_axis=0, concat_axis=0, tiled=True)
    return arrived


def refresh(block_grads, left_stats, right_stats):
    gram_left = jnp.einsum(
        "kij,klj->kil", block_grads, block_grads, preferred_element_type=jnp.float32
    )
    new_left = stat_decay * left_stats + (1.0 - stat_decay) * gram_left
    gram_right = jnp.einsum(
        "kji,kjl->kil", block_grads, block_grads, preferred_element_type=jnp.float32
    )
    new_right = stat_decay * right_stats + (1.0 - stat_decay) * gram_right
    return (new_left, new_right)


def direction(block_grads, left_root, right_root, moment):
    half = jnp.einsum(
        "kij,kjl->kil", left_root, block_grads, preferred_element_type=jnp.float32
    ).astype(jnp.bfloat16)
    precond = jnp.einsum("kij,kjl->kil", half, right_root, preferred_element_type=jnp.float32)
    grad_full = block_grads.astype(jnp.float32)
    new_moment = stat_decay * moment + (1.0 - stat_decay) * grad_full * grad_full
    adam = grad_full / (jnp.sqrt(new_moment) + 1e-08)
    graft = jnp.sqrt(jnp.mean(adam * adam, axis=(1, 2))) / jnp.sqrt(
        jnp.mean(precond * precond, axis=(1, 2)) + 1e-06
    )
    delta = (graft[:, None, None] * precond).astype(jnp.bfloat16)
    return (delta, new_moment)


def body_steps(weights, grads, owner_slot, left_stats, right_stats, left_root, right_root, moment):
    n_shard = lax.axis_size("shard")
    n_tensor = lax.axis_size("tensor")
    row_blocks, shard_rows, shard_cols = grads.shape
    order_size = left_stats.shape[1]
    width = shard_cols * n_tensor
    col_blocks = width // order_size
    per_block = n_tensor // col_blocks
    slots = left_stats.shape[0]
    owners = n_shard * n_tensor
    total_slots = owners * slots
    half = shard_rows // col_blocks
    mine_col = lax.axis_index("tensor") // per_block
    partner = [(i, (i + per_block) % n_tensor) for i in range(n_tensor)]
    keep = lax.dynamic_slice_in_dim(grads, mine_col * half, half, axis=1)
    give = lax.dynamic_slice_in_dim(grads, (1 - mine_col) * half, half, axis=1)
    got = lax.ppermute(give, "tensor", partner)
    first = jnp.where(mine_col == 0, keep, got)
    second = jnp.where(mine_col == 0, got, keep)
    block_count = owner_slot.shape[0]
    slab_size = half * shard_cols
    chunk = slots * slab_size
    lanes = 128 if chunk % 128 == 0 else chunk
    slabs = jnp.stack([first, second], axis=1).reshape(row_blocks * col_blocks, slab_size)
    slot_block = jnp.zeros((total_slots,), jnp.int32).at[owner_slot].set(
        jnp.arange(block_count, dtype=jnp.int32)
    )
    slot_used = jnp.zeros((total_slots,), jnp.bool_).at[owner_slot].set(True)
    lane_rows = slab_size // lanes
    chunk_rows = chunk // lanes
    padded_rows = -(-chunk_rows // 8) * 8
    flat = slabs.reshape(row_blocks * col_blocks * lane_rows, lanes)
    blank = flat.shape[0]
    flat = jnp.concatenate([flat, jnp.zeros((1, lanes), jnp.bfloat16)], axis=0)
    rows_q = jnp.arange(padded_rows)
    slot_g = jnp.minimum(
        jnp.arange(owners)[:, None] * slots + (rows_q // lane_rows)[None, :], total_slots - 1
    )
    valid = (rows_q < chunk_rows)[None, :] & slot_used[slot_g]
    source_row = jnp.where(valid, slot_block[slot_g] * lane_rows + (rows_q % lane_rows)[None, :], blank)
    arrived = route_out(flat[source_row])[:, :chunk_rows]
    arrived = arrived.reshape(n_shard, col_blocks, per_block, slots, half, shard_cols)
    block_grads = arrived.transpose(3, 0, 1, 4, 2, 5).reshape(slots, order_size, order_size)
    new_left, new_right = refresh(block_grads, left_stats, right_stats)
    delta, new_moment = direction(block_grads, left_root, right_root, moment)
    pieces = delta.reshape(slots, n_shard, col_blocks, half, per_block, shard_cols).transpose(
        1, 2, 4, 0, 3, 5
    )
    sendback = pieces.reshape(owners, chunk // lanes, lanes)
    returned = route_back(sendback).reshape(total_slots, slab_size)
    back = returned[owner_slot].reshape(row_blocks, col_blocks, half, shard_cols)
    own_part = jnp.where(mine_col == 0, back[:, 0], back[:, 1])
    other_part = jnp.where(mine_col == 0, back[:, 1], back[:, 0])
    other_back = lax.ppermute(other_part, "tensor", partner)
    top = jnp.where(mine_col == 0, own_part, other_back)
    bottom = jnp.where(mine_col == 0, other_back, own_part)
    my_delta = jnp.concatenate([top, bottom], axis=1)
    updated = weights - step_size * my_delta.astype(jnp.float32)
    squares = jnp.sum(updated * updated, axis=2)
    step = 1
    while step < n_tensor:
        pairs = [(i, i ^ step) for i in range(n_tensor)]
        squares = squares + lax.ppermute(squares, "tensor", pairs)
        step *= 2
    new_weights = updated * lax.rsqrt(squares / width + 1e-06)[:, :, None]
    return (new_weights, new_left, new_right, new_moment)


def solution(mesh):
    placed = (
        P(None, "shard", "tensor"),
        P(None, "shard", "tensor"),
        P(),
        P(("shard", "tensor"), None, None),
        P(("shard", "tensor"), None, None),
        P(("shard", "tensor"), None, None),
        P(("shard", "tensor"), None, None),
        P(("shard", "tensor"), None, None),
    )
    return jax.shard_map(
        body_steps,
        mesh=mesh,
        in_specs=placed,
        out_specs=(
            P(None, "shard", "tensor"),
            P(("shard", "tensor"), None, None),
            P(("shard", "tensor"), None, None),
            P(("shard", "tensor"), None, None),
        ),
        check_vma=False,
    )
```

```python
import jax
import jax.numpy as jnp
from jax import lax
from jax.sharding import PartitionSpec as P

stat_decay = 0.9
step_size = 0.2


def route_out(outgoing):
    arrived = lax.all_to_all(outgoing, ("shard", "tensor"), split_axis=0, concat_axis=0, tiled=True)
    return arrived


def route_back(outgoing):
    arrived = lax.all_to_all(outgoing, ("shard", "tensor"), split_axis=0, concat_axis=0, tiled=True)
    return arrived


def refresh(block_grads, left_stats, right_stats):
    gram_left = jnp.einsum(
        "kij,klj->kil", block_grads, block_grads, preferred_element_type=jnp.float32
    )
    new_left = stat_decay * left_stats + (1.0 - stat_decay) * gram_left
    gram_right = jnp.einsum(
        "kji,kjl->kil", block_grads, block_grads, preferred_element_type=jnp.float32
    )
    new_right = stat_decay * right_stats + (1.0 - stat_decay) * gram_right
    return (new_left, new_right)


def direction(block_grads, left_root, right_root, moment):
    half = jnp.einsum(
        "kij,kjl->kil", left_root, block_grads, preferred_element_type=jnp.float32
    ).astype(jnp.bfloat16)
    precond = jnp.einsum("kij,kjl->kil", half, right_root, preferred_element_type=jnp.float32)
    grad_full = block_grads.astype(jnp.float32)
    new_moment = stat_decay * moment + (1.0 - stat_decay) * grad_full * grad_full
    adam = grad_full / (jnp.sqrt(new_moment) + 1e-08)
    graft = jnp.sqrt(jnp.mean(adam * adam, axis=(1, 2))) / jnp.sqrt(
        jnp.mean(precond * precond, axis=(1, 2)) + 1e-06
    )
    delta = (graft[:, None, None] * precond).astype(jnp.bfloat16)
    return (delta, new_moment)


def body_steps(weights, grads, owner_slot, left_stats, right_stats, left_root, right_root, moment):
    n_shard = lax.axis_size("shard")
    n_tensor = lax.axis_size("tensor")
    row_blocks, shard_rows, shard_cols = grads.shape
    order_size = left_stats.shape[1]
    width = shard_cols * n_tensor
    col_blocks = width // order_size
    per_block = n_tensor // col_blocks
    slots = left_stats.shape[0]
    owners = n_shard * n_tensor
    total_slots = owners * slots
    half = shard_rows // col_blocks
    mine_col = lax.axis_index("tensor") // per_block
    partner = [(i, (i + per_block) % n_tensor) for i in range(n_tensor)]
    keep = lax.dynamic_slice_in_dim(grads, mine_col * half, half, axis=1)
    give = lax.dynamic_slice_in_dim(grads, (1 - mine_col) * half, half, axis=1)
    got = lax.ppermute(give, "tensor", partner)
    block_count = owner_slot.shape[0]
    slab_size = half * shard_cols
    chunk = slots * slab_size
    lanes = 128 if chunk % 128 == 0 else chunk
    slabs = jnp.stack([keep, got], axis=1).reshape(row_blocks * col_blocks, slab_size)
    slot_block = jnp.zeros((total_slots,), jnp.int32).at[owner_slot].set(
        jnp.arange(block_count, dtype=jnp.int32)
    )
    slot_used = jnp.zeros((total_slots,), jnp.bool_).at[owner_slot].set(True)
    slab_index = (slot_block // col_blocks) * col_blocks + (slot_block % col_blocks != mine_col)
    outgoing = jnp.where(slot_used[:, None], slabs[slab_index], jnp.zeros((), jnp.bfloat16))
    arrived = route_out(outgoing.reshape(owners, chunk // lanes, lanes))
    arrived = arrived.reshape(n_shard, col_blocks, per_block, slots, half, shard_cols)
    block_grads = arrived.transpose(3, 0, 1, 4, 2, 5).reshape(slots, order_size, order_size)
    new_left, new_right = refresh(block_grads, left_stats, right_stats)
    delta, new_moment = direction(block_grads, left_root, right_root, moment)
    pieces = delta.reshape(slots, n_shard, col_blocks, half, per_block, shard_cols).transpose(
        1, 2, 4, 0, 3, 5
    )
    sendback = pieces.reshape(owners, chunk // lanes, lanes)
    returned = route_back(sendback).reshape(total_slots, slab_size)
    back = returned[owner_slot].reshape(row_blocks, col_blocks, half, shard_cols)
    own_part = jnp.where(mine_col == 0, back[:, 0], back[:, 1])
    other_part = jnp.where(mine_col == 0, back[:, 1], back[:, 0])
    other_back = lax.ppermute(other_part, "tensor", partner)
    top = jnp.where(mine_col == 0, own_part, other_back)
    bottom = jnp.where(mine_col == 0, other_back, own_part)
    my_delta = jnp.concatenate([top, bottom], axis=1)
    updated = weights - step_size * my_delta.astype(jnp.float32)
    squares = jnp.sum(updated * updated, axis=2)
    step = 1
    while step < n_tensor:
        pairs = [(i, i ^ step) for i in range(n_tensor)]
        squares = squares + lax.ppermute(squares, "tensor", pairs)
        step *= 2
    new_weights = updated * lax.rsqrt(squares / width + 1e-06)[:, :, None]
    return (new_weights, new_left, new_right, new_moment)


def solution(mesh):
    placed = (
        P(None, "shard", "tensor"),
        P(None, "shard", "tensor"),
        P(),
        P(("shard", "tensor"), None, None),
        P(("shard", "tensor"), None, None),
        P(("shard", "tensor"), None, None),
        P(("shard", "tensor"), None, None),
        P(("shard", "tensor"), None, None),
    )
    return jax.shard_map(
        body_steps,
        mesh=mesh,
        in_specs=placed,
        out_specs=(
            P(None, "shard", "tensor"),
            P(("shard", "tensor"), None, None),
            P(("shard", "tensor"), None, None),
            P(("shard", "tensor"), None, None),
        ),
        check_vma=False,
    )
```
